32 devices in a mesh: seq: 4 (over z), head: 4 (over y, x), rep: 2 (over core).
Axes of the slice: x: 2, y: 2, z: 4, core: 2. Of those that a mesh axis runs over, the one named last changes fastest.
Arguments:
- queries: bfloat16 [1024, 8, 128], P(('rep', 'seq'), 'head'), parts along dimension 0, may hold values from -8 to 8
- keys: bfloat16 [1024, 128], P(('rep', 'seq')), parts along dimension 0, may hold values from -8 to 8
- values: bfloat16 [1024, 128], P(('rep', 'seq')), parts along dimension 0, may hold values from -6 to 6
- query_weight: float32 [16, 64, 128], P(('rep', 'head')), parts along dimension 0, may hold values from -0.075 to 0.075
- key_weight: float32 [16, 64, 128], P(('rep', 'head')), parts along dimension 0, may hold values from -0.075 to 0.075
Outputs:
- loss: float32 [2], P('rep'), parts along dimension 0
- grad_query_weight: float32 [16, 64, 128], P(('rep', 'head')), parts along dimension 0
- grad_key_weight: float32 [16, 64, 128], P(('rep', 'head')), parts along dimension 0
The draws below stay inside these ranges and needn't reach their ends.
There are 2 independent parts, one for each index of `rep`. The reference program is written for one: setup_inputs(seed, part) draws one part's arguments, and reference() takes and returns one part's arrays. A program takes and returns all parts, laid end to end along the dimension named above; each array names one. Nothing has to cross between parts.
All inputs are finite; a program needn't handle non-finite values.
Results may differ from the reference program's by a relative error of at most 0.00045.
Values may be sent and summed in bfloat16 or wider, within the bound.
No kernel may reach another device: no remote copies, remote signals or barrier semaphores. Data moves between devices by JAX's collectives and lax.ppermute only.
A program may use at most 64 MiB of HBM per device.

```python
import math
import jax
import jax.numpy as jnp
from jax import lax

DH = 128
HEADS = 8
FH = 64
WINDOW = 64
TOK_DEV = 128
TOKENS = 512


def drawn_pair(key):
    base = jax.random.fold_in(key, 4242)
    pick_query, pick_key = jax.random.split(base, 2)
    queries = 1.7 * jax.random.truncated_normal(pick_query, -4.5, 4.5, (TOKENS, HEADS, DH), jnp.float32)
    keys = 1.7 * jax.random.truncated_normal(pick_key, -4.5, 4.5, (TOKENS, DH), jnp.float32)
    return (queries, keys)


def draw_queries(key, part):
    return drawn_pair(key)[0].astype(jnp.bfloat16)


def draw_keys(key, part):
    return drawn_pair(key)[1].astype(jnp.bfloat16)


def shard_levels(own_key, dims, shards, smallest, high):
    gain = 1.0
    for axis_at, parts in shards:
        heights = jax.random.uniform(jax.random.fold_in(jax.random.fold_in(own_key, 6), axis_at), (parts,), jnp.float32, smallest / len(shards), high / len(shards))
        gain = gain * jnp.repeat(jnp.exp(heights), dims[axis_at] // parts).reshape((-1,) + (1,) * (len(dims) - 1 - axis_at))
    return gain


def gaussian(own_key, dims, spread, reach, cuts=(), kind=jnp.bfloat16):
    loudness = shard_levels(own_key, dims, cuts, -0.22, 0.18) if cuts else 1.0
    drawn = jax.random.normal(own_key, dims, jnp.float32) * spread * loudness
    return jnp.minimum(jnp.maximum(drawn, -reach), reach).astype(kind)


def setup_inputs(seed: int = 0, part: int = 0) -> dict:
    streams_of = jax.random.split(jax.random.key(seed), 6)
    own_keys = jax.random.split(jax.random.fold_in(streams_of[5], part), 6)
    return {
        "queries": draw_queries(jax.random.fold_in(jax.random.fold_in(streams_of[5], part), 71), part),
        "keys": draw_keys(jax.random.fold_in(jax.random.fold_in(streams_of[5], part), 71), part),
        "values": gaussian(own_keys[2], (TOKENS, DH), 1.0, 6.0, ((0, 4),)),
        "query_weight": jnp.clip(jax.random.uniform(own_keys[3], (HEADS, FH, DH), jnp.float32, -0.075, 0.075) * shard_levels(own_keys[3], (HEADS, FH, DH), ((0, 4),), -0.4, 0.0), -0.075, 0.075),
        "key_weight": jnp.clip(jax.random.uniform(own_keys[4], (HEADS, FH, DH), jnp.float32, -0.075, 0.075) * shard_levels(own_keys[4], (HEADS, FH, DH), ((0, 4),), -0.4, 0.0), -0.075, 0.075),
    }


very_low = -1.0e30
exact = lax.Precision.HIGHEST


def feature_map(act):
    first = jnp.exp(act)
    second = jnp.exp(-act)
    return jnp.concatenate([first / jnp.sum(first, axis=-1, keepdims=True), second / jnp.sum(second, axis=-1, keepdims=True)], axis=-1)


def feature_back(features, grad):
    half = features.shape[-1] // 2
    first = features[..., :half]
    second = features[..., half:]
    grad_first = grad[..., :half]
    grad_second = grad[..., half:]
    return first * (grad_first - jnp.sum(first * grad_first, axis=-1, keepdims=True)) - second * (grad_second - jnp.sum(second * grad_second, axis=-1, keepdims=True))


def rounded(array):
    return lax.optimization_barrier(array.astype(jnp.bfloat16)).astype(jnp.float32)


def reference(queries, keys, values, query_weight, key_weight):
    width = queries.shape[2]
    scale = width ** -0.5
    block = math.gcd(TOK_DEV, 128)
    queries_wide = queries.astype(jnp.float32)
    keys_wide = keys.astype(jnp.float32)
    values_wide = values.astype(jnp.float32)
    key_features = feature_map(jnp.einsum('jd,hfd->hjf', keys_wide, key_weight, precision=exact))
    key_place = jnp.arange(TOKENS, dtype=jnp.int32)

    def one_block(carry, start):
        loss_sum, key_grad, query_grad = carry
        query_block = lax.dynamic_slice_in_dim(queries_wide, start, block, 0)
        query_place = start + jnp.arange(block, dtype=jnp.int32)
        scores = jnp.einsum('thd,jd->htj', query_block, keys_wide, precision=exact) * scale
        causal = (key_place[None, :] <= query_place[:, None])[None]
        teacher_best = jnp.max(jnp.where(causal, scores, very_low), axis=-1)
        teacher_weights = jnp.where(causal, jnp.exp(scores - teacher_best[..., None]), 0.0)
        teacher_total = jnp.sum(teacher_weights, axis=-1)
        teacher_sum = jnp.einsum('htj,jd->htd', rounded(teacher_weights), values_wide, precision=exact)
        teacher = rounded(teacher_sum / teacher_total[..., None])
        window = causal & (key_place[None, :] > query_place[:, None] - WINDOW)[None]
        linear_mask = (key_place[None, :] <= query_place[:, None] - WINDOW)[None]
        window_best = jnp.max(jnp.where(window, scores, very_low), axis=-1)
        window_weights = jnp.where(window, jnp.exp(scores - window_best[..., None]), 0.0)
        window_total = jnp.sum(window_weights, axis=-1)
        window_sum = jnp.einsum('htj,jd->htd', rounded(window_weights), values_wide, precision=exact)
        query_features = feature_map(jnp.einsum('thd,hfd->htf', query_block, query_weight, precision=exact))
        linear = jnp.where(linear_mask, jnp.einsum('htf,hjf->htj', query_features, key_features, precision=exact), 0.0)
        linear_sum = jnp.einsum('htj,jd->htd', linear, values_wide, precision=exact)
        linear_total = jnp.sum(linear, axis=-1)
        lift = jnp.exp(-window_best)
        denominator = window_total + lift * linear_total
        student = (window_sum + lift[..., None] * linear_sum) / denominator[..., None]
        difference = student - teacher
        loss_sum = loss_sum + jnp.sum(difference * difference) / TOKENS
        grad_out = 2.0 * difference / TOKENS
        num_grad = lift[..., None] * grad_out / denominator[..., None]
        den_grad = -lift * jnp.sum(grad_out * student, axis=-1) / denominator
        link = jnp.where(linear_mask, jnp.einsum('htd,jd->htj', num_grad, values_wide, precision=exact) + den_grad[..., None], 0.0)
        query_feature_grad = jnp.einsum('htj,hjf->htf', link, key_features, precision=exact)
        key_grad = key_grad + jnp.einsum('htj,htf->hjf', link, query_features, precision=exact)
        query_act_grad = feature_back(query_features, query_feature_grad)
        query_grad = query_grad + jnp.einsum('htf,thd->hfd', query_act_grad, query_block, precision=exact)
        return (loss_sum, key_grad, query_grad), None

    init = (jnp.zeros((), jnp.float32), jnp.zeros(key_features.shape, jnp.float32), jnp.zeros(query_weight.shape, jnp.float32))
    starts = jnp.arange(0, TOKENS, block, dtype=jnp.int32)
    (loss_sum, key_grad, query_grad), unused = lax.scan(one_block, init, starts)
    key_act_grad = feature_back(key_features, key_grad)
    grad_key = jnp.einsum('hjf,jd->hfd', key_act_grad, keys_wide, precision=exact)
    return loss_sum.reshape(1), query_grad, grad_key
```

```python
import functools

import jax
import jax.numpy as jnp
from jax import lax
from jax.experimental import pallas as pl
from jax.experimental.pallas import tpu as pltpu
from jax.sharding import PartitionSpec as P

WINDOW = 64


very_low = -1e30
exact = lax.Precision.HIGHEST
f32, bf16 = jnp.float32, jnp.bfloat16
PAD = 16
LIMIT = 8


def shifted(value, axis, steps):
    count = lax.axis_size(axis)
    leading, last = (max(0, -steps), min(count, count - steps))
    return lax.ppermute(value, axis, [(source, source + steps) for source in range(leading, last)])


def prefix_2(x, axis, combine, identity):
    peers, place = (lax.axis_size(axis), lax.axis_index(axis))
    everything = jax.tree.map(lambda part: lax.all_gather(part, axis), x)
    start = jax.tree.map(
        lambda part, zero: jnp.broadcast_to(jnp.asarray(zero, part.dtype), part.shape), x, identity
    )

    def lap(k, before):
        at = peers - 1 - k
        reached = at > place
        new = combine(before, jax.tree.map(lambda part: part[at], everything))
        return jax.tree.map(lambda a, b: jnp.where(reached, a, b), new, before)

    return lax.fori_loop(0, peers, lap, start)


def feature_map(act):
    first = jnp.exp(act)
    second = jnp.exp(-act)
    return jnp.concatenate(
        [
            first / jnp.sum(first, axis=-1, keepdims=True),
            second / jnp.sum(second, axis=-1, keepdims=True),
        ],
        axis=-1,
    )


def feature_back(features, grad):
    half = features.shape[-1] // 2
    first = features[..., :half]
    second = features[..., half:]
    grad_first = grad[..., :half]
    grad_second = grad[..., half:]
    return first * (grad_first - jnp.sum(first * grad_first, axis=-1, keepdims=True)) - second * (
        grad_second - jnp.sum(second * grad_second, axis=-1, keepdims=True)
    )


def key_feature_map(keys_wide, key_weight):
    return feature_map(jnp.einsum("jd,hfd->hjf", keys_wide, key_weight, precision=exact))


def add_pair(earlier, later):
    return (earlier[0] + later[0], earlier[1] + later[1])


def flash_update(carry, queries, keys, values, query_place, key_place):
    best, total, accum = carry
    scale = queries.shape[-1] ** (-0.5)
    scores = jnp.einsum("thd,jd->htj", queries, keys, preferred_element_type=jnp.float32) * scale
    allowed = (key_place[None, :] <= query_place[:, None])[None]
    scores = jnp.where(allowed, scores, very_low)
    fresh = jnp.maximum(best, jnp.max(scores, axis=-1))
    weights = jnp.where(allowed, jnp.exp(scores - fresh[..., None]), 0.0)
    total = jnp.sum(weights, axis=-1)
    accum = jnp.einsum(
        "htj,jd->htd", weights.astype(jnp.bfloat16), values, preferred_element_type=jnp.float32
    )
    return (fresh, total, accum)


def state_update(state, keys, values, key_place, bound, key_weight):

    def accumulate(inner):
        keep = (key_place < bound).astype(jnp.float32)
        features = key_feature_map(keys.astype(jnp.float32), key_weight) * keep[None, :, None]
        return (
            jnp.einsum("hjf,jd->hfd", features, values.astype(jnp.float32), precision=exact),
            jnp.sum(features, axis=1),
        )

    return lax.cond(jnp.min(key_place) < bound, accumulate, lambda inner: inner, state)


def local_general(queries, keys, values, query_weight, key_weight):
    rows, local_heads, width = queries.shape
    shards = lax.axis_size("seq")
    device = lax.axis_index("seq")
    feature_count = 2 * query_weight.shape[1]
    total_tokens = rows * shards
    first_place = device * rows
    bound = first_place - WINDOW
    natural_place = first_place + jnp.arange(rows, dtype=jnp.int32)
    flash_init = (
        jnp.full((local_heads, rows), very_low, jnp.float32),
        jnp.zeros((local_heads, rows), jnp.float32),
        jnp.zeros((local_heads, rows, width), jnp.float32),
    )
    zero_state = (
        jnp.zeros((local_heads, feature_count, width), jnp.float32),
        jnp.zeros((local_heads, feature_count), jnp.float32),
    )
    halo_keys, halo_values = shifted((keys[rows - WINDOW :], values[rows - WINDOW :]), "seq", 1)
    ext_keys = jnp.concatenate([halo_keys, keys], axis=0)
    ext_values = jnp.concatenate([halo_values, values], axis=0)
    ext_count = rows + WINDOW
    ext_place = bound + jnp.arange(ext_count, dtype=jnp.int32)
    valid = ext_place >= 0
    covered = jnp.arange(ext_count, dtype=jnp.int32) < rows
    cover_mask = (valid & covered).astype(jnp.float32)
    ext_keys_wide = ext_keys.astype(jnp.float32)
    ext_values_wide = ext_values.astype(jnp.float32)
    key_features = key_feature_map(ext_keys_wide, key_weight)
    fold_keys, fold_values = (keys, values)
    piece_keys = lax.all_gather(fold_keys, "seq", axis=0, tiled=True)
    piece_values = lax.all_gather(fold_values, "seq", axis=0, tiled=True)
    key_place = jnp.arange(piece_keys.shape[0], dtype=jnp.int32)

    def attend(inner):
        flash = flash_update(inner[0], queries, piece_keys, piece_values, natural_place, key_place)
        state = state_update(inner[1], piece_keys, piece_values, key_place, bound, key_weight)
        return (flash, state)

    flash, folded = lax.cond(
        jnp.int32(0) < first_place + rows, attend, lambda inner: inner, (flash_init, zero_state)
    )
    teacher = jnp.transpose(flash[2] / flash[1][..., None], (1, 0, 2)).astype(jnp.bfloat16)
    scale = width ** (-0.5)
    scores = (
        jnp.einsum("thd,jd->htj", queries, ext_keys, preferred_element_type=jnp.float32) * scale
    )
    window = (
        (ext_place[None, :] <= natural_place[:, None])
        & (ext_place[None, :] > natural_place[:, None] - WINDOW)
        & valid[None, :]
    )[None]
    linear_mask = ((ext_place[None, :] <= natural_place[:, None] - WINDOW) & valid[None, :])[None]
    window_best = jnp.max(jnp.where(window, scores, very_low), axis=-1)
    window_weights = jnp.where(window, jnp.exp(scores - window_best[..., None]), 0.0)
    window_total = jnp.sum(window_weights, axis=-1)
    window_sum = jnp.einsum(
        "htj,jd->htd",
        window_weights.astype(jnp.bfloat16),
        ext_values,
        preferred_element_type=jnp.float32,
    )
    queries_wide = queries.astype(jnp.float32)
    query_features = feature_map(
        jnp.einsum("thd,hfd->htf", queries_wide, query_weight, precision=exact)
    )
    linear = jnp.where(
        linear_mask, jnp.einsum("htf,hjf->htj", query_features, key_features, precision=exact), 0.0
    )
    linear_sum = jnp.einsum("htj,jd->htd", linear, ext_values_wide, precision=exact) + jnp.einsum(
        "htf,hfd->htd", query_features, folded[0], precision=exact
    )
    linear_total = jnp.sum(linear, axis=-1) + jnp.einsum(
        "htf,hf->ht", query_features, folded[1], precision=exact
    )
    lift = jnp.exp(-window_best)
    denominator = window_total + lift * linear_total
    student = (window_sum + lift[..., None] * linear_sum) / denominator[..., None]
    teacher_wide = jnp.transpose(teacher, (1, 0, 2)).astype(jnp.float32)
    difference = student - teacher_wide
    loss_part = jnp.sum(difference * difference) / total_tokens
    grad_out = 2.0 * difference / total_tokens
    num_grad = lift[..., None] * grad_out / denominator[..., None]
    den_grad = -lift * jnp.sum(grad_out * student, axis=-1) / denominator
    adjoint = (
        jnp.einsum("htf,htd->hfd", query_features, num_grad, precision=exact),
        jnp.einsum("htf,ht->hf", query_features, den_grad, precision=exact),
    )
    later = prefix_2(adjoint, "seq", add_pair, zero_state)
    link = jnp.where(
        linear_mask,
        jnp.einsum("htd,jd->htj", num_grad, ext_values_wide, precision=exact) + den_grad[..., None],
        0.0,
    )
    query_feature_grad = (
        jnp.einsum("htj,hjf->htf", link, key_features, precision=exact)
        + jnp.einsum("htd,hfd->htf", num_grad, folded[0], precision=exact)
        + den_grad[..., None] * folded[1][:, None, :]
    )
    key_feature_grad = (
        jnp.einsum("htj,htf->hjf", link, query_features, precision=exact)
        + jnp.einsum("jd,hfd->hjf", ext_values_wide, later[0], precision=exact)
        + later[1][:, None, :]
    )
    key_feature_grad = key_feature_grad * cover_mask[None, :, None]
    query_act_grad = feature_back(query_features, query_feature_grad)
    key_act_grad = feature_back(key_features, key_feature_grad)
    grad_query = jnp.einsum("htf,thd->hfd", query_act_grad, queries_wide, precision=exact)
    grad_key = jnp.einsum("hjf,jd->hfd", key_act_grad, ext_keys_wide, precision=exact)
    grad_query, grad_key = lax.psum((grad_query, grad_key), "seq")
    loss = lax.psum(loss_part, ("seq", "head")).reshape(1)
    return (loss, grad_query, grad_key)


def dot(a, b):
    return lax.dot_general(a, b, (((1,), (0,)), ((), ())), preferred_element_type=f32)


def dot_t(a, b):
    return lax.dot_general(a, b, (((1,), (1,)), ((), ())), preferred_element_type=f32)


def split(x):
    high = x.astype(bf16)
    return high, (x - high.astype(f32)).astype(bf16)


def dot3(a, b):
    return dot(a[0], b[0]) + (dot(a[0], b[1]) + dot(a[1], b[0]))


def dot_left(a, b):
    return dot(a[0], b) + dot(a[1], b)


def dot_right(a, b):
    return dot(a, b[0]) + dot(a, b[1])


def iota(shape, axis):
    return lax.broadcasted_iota(jnp.int32, shape, axis)


def head_pass(queries, keys, values, ext_keys, ext_values, ext_keys_t, values_t, ext_aug_t, ext_aug, pair_sum, query_weight, key_weight, block, tokens_total):
    tokens, width = queries.shape
    blocks = tokens // block
    scale = width ** (-0.5)
    wq = split(jnp.concatenate([query_weight, -query_weight], axis=0))
    wk = split(jnp.concatenate([key_weight, -key_weight], axis=0))
    raised_t = jnp.exp(dot_t(wq[0], queries) + dot_t(wq[1], queries))
    qf_t = raised_t / dot_right(pair_sum, split(raised_t))
    raised = jnp.exp(dot_t(ext_keys, wk[0]) + dot_t(ext_keys, wk[1]))
    kf = raised / dot_left(split(raised), pair_sum)
    kf = jnp.where(iota(kf.shape, 0) >= WINDOW, kf, 0.0)
    qf = qf_t.T
    kf_t = kf.T
    qf_ts, kf_s, qf_s, kf_ts = split(qf_t), split(kf), split(qf), split(kf_t)
    tri = iota((block, block), 0) <= iota((block, block), 1)
    near = iota((block + WINDOW, block), 0) > iota((block + WINDOW, block), 1)
    loss = jnp.zeros((1, 1), f32)
    state_t = None
    state = None
    saved = []
    cut = lambda pair, at: tuple(part[at] for part in pair)
    for b in range(blocks):
        lo, hi = b * block, (b + 1) * block
        here = (slice(None), slice(lo, hi))
        rows = (slice(lo, hi), slice(None))
        scores = dot_t(keys[:hi], queries[lo:hi]) * scale
        tail = scores[lo:]
        causal = jnp.where(tri, tail, very_low)
        best = jnp.max(causal, axis=0, keepdims=True)
        if b:
            best = jnp.maximum(best, jnp.max(scores[:lo], axis=0, keepdims=True))
        weights = jnp.where(tri, jnp.exp(tail - best), 0.0)
        total = jnp.sum(weights, axis=0, keepdims=True)
        teacher = dot(values_t[:, lo:hi], weights.astype(bf16))
        if b:
            weights = jnp.exp(scores[:lo] - best)
            total = total + jnp.sum(weights, axis=0, keepdims=True)
            teacher = teacher + dot(values_t[:, :lo], weights.astype(bf16))
        teacher = (teacher / total).astype(bf16).astype(f32)
        inside = tri & near[WINDOW:]
        wbest = jnp.max(jnp.where(inside, tail, very_low), axis=0, keepdims=True)
        if b:
            early = jnp.where(near[:WINDOW], scores[lo - WINDOW : lo], very_low)
            wbest = jnp.maximum(wbest, jnp.max(early, axis=0, keepdims=True))
        weights = jnp.where(inside, jnp.exp(tail - wbest), 0.0)
        wtotal = jnp.sum(weights, axis=0, keepdims=True)
        wsum = dot(values_t[:, lo:hi], weights.astype(bf16))
        if b:
            weights = jnp.where(near[:WINDOW], jnp.exp(early - wbest), 0.0)
            wtotal = wtotal + jnp.sum(weights, axis=0, keepdims=True)
            weights = jnp.concatenate([jnp.zeros((128 - WINDOW, block), bf16), weights.astype(bf16)], axis=0)
            wsum = wsum + dot(values_t[:, lo - 128 : lo], weights)
        linear = jnp.where(tri, dot3(cut(kf_s, rows), cut(qf_ts, here)), 0.0)
        aug = dot_right(ext_aug_t[:, lo:hi], split(linear))
        if b:
            aug = aug + dot3(split(state_t), cut(qf_ts, here))
        saved_state = state
        if b + 1 < blocks:
            grown_t = dot_right(ext_aug_t[:, lo:hi], cut(kf_s, rows))
            grown = dot_left(cut(kf_ts, here), ext_aug[lo:hi])
            state_t = grown_t if state_t is None else state_t + grown_t
            state = grown if state is None else state + grown
        lift = jnp.exp(-wbest)
        over = 1.0 / (wtotal + lift * aug[width : width + 1])
        student = (wsum + lift * aug[:width]) * over
        difference = student - teacher
        loss = loss + jnp.sum(jnp.sum(difference * difference, axis=0, keepdims=True), axis=1, keepdims=True)
        grad = difference * (2.0 / tokens_total)
        num = grad * (lift * over)
        den = -(lift * over) * jnp.sum(grad * student, axis=0, keepdims=True)
        saved.append((num, den, saved_state))
    grad_q = jnp.zeros((qf_t.shape[0], width), f32)
    grad_k = jnp.zeros((width, kf.shape[1]), f32)
    later = None
    for b in reversed(range(blocks)):
        lo, hi = b * block, (b + 1) * block
        here = (slice(None), slice(lo, hi))
        rows = (slice(lo, hi), slice(None))
        num, den, state_b = saved[b]
        num_s = split(num)
        link = jnp.where(tri, dot_right(ext_values[lo:hi], num_s) + den, 0.0)
        link_s = split(link)
        qfg = dot3(cut(kf_ts, here), link_s)
        if b:
            qfg = qfg + dot3(split(state_b[:, :width]), num_s) + state_b[:, width : width + 1] * den
        kfg = dot3(link_s, cut(qf_s, rows))
        if later is not None:
            kfg = kfg + dot_right(ext_values[lo:hi], split(later[:width])) + later[width : width + 1]
        if b:
            fill = jnp.concatenate([num, den, jnp.zeros((PAD - 1, block), f32)], axis=0)
            grown = dot3(split(fill), cut(qf_s, rows))
            later = grown if later is None else later + grown
        f_t = qf_t[here]
        back = f_t * (qfg - dot_right(pair_sum, split(f_t * qfg)))
        grad_q = grad_q + dot_left(split(back), queries[lo:hi])
        f = kf[rows]
        back = f * (kfg - dot_left(split(f * kfg), pair_sum))
        grad_k = grad_k + dot_right(ext_keys_t[:, lo:hi], split(back))
    half = grad_q.shape[0] // 2
    grad_k = grad_k.T
    return loss, grad_q[:half] - grad_q[half:], grad_k[:half] - grad_k[half:]


def shared_parts(keys, values, ext_keys, ext_values, features):
    tokens, width = keys.shape
    eye = (iota((width, width), 0) == iota((width, width), 1)).astype(bf16)
    turn = lambda x: dot_t(eye, x).astype(bf16)
    values_t = turn(values)
    ext_keys_t = turn(ext_keys)
    ones = (iota((PAD, tokens), 0) == 0).astype(bf16)
    ext_aug_t = jnp.concatenate([turn(ext_values), ones], axis=0)
    ext_aug = jnp.concatenate([ext_values, (iota((tokens, width), 1) == 0).astype(bf16)], axis=1)
    half = features // 2
    pair_sum = ((iota((features, features), 0) < half) == (iota((features, features), 1) < half)).astype(bf16)
    return values_t, ext_keys_t, ext_aug_t, ext_aug, pair_sum


def pack_kernel(queries_ref, keys_ref, values_ref, same_ref, other_ref):
    rows = keys_ref.shape[0]
    odd = lax.rem(lax.axis_index("seq"), 2) == 1
    first, second = queries_ref[:, 0, :], queries_ref[:, 1, :]
    for ref, chosen in ((same_ref, jnp.where(odd, second, first)), (other_ref, jnp.where(odd, first, second))):
        ref[:rows] = keys_ref[...]
        ref[rows : 2 * rows] = values_ref[...]
        ref[2 * rows :] = chosen


def main_kernel(shards, rows, *refs):
    blocks_in = refs[:shards]
    query_weight_ref, key_weight_ref, grads_ref, loss_ref, keys_ref, values_ref, queries_ref, qw_ref, kw_ref, sems = refs[shards:]
    tokens, width = queries_ref.shape
    place = lax.axis_index("seq")
    mine = lax.rem(place, 2)
    copies = []
    for d in range(shards):
        source = lax.rem(place + shards - d, shards)
        at = pl.multiple_of(source * rows, rows)
        for k, (ref, offset) in enumerate(((keys_ref, WINDOW), (values_ref, WINDOW), (queries_ref, 0))):
            copies.append(
                pltpu.make_async_copy(
                    blocks_in[d].at[pl.ds(k * rows, rows)], ref.at[pl.ds(at + offset, rows)], sems.at[3 * d + k]
                )
            )
    copies.append(pltpu.make_async_copy(query_weight_ref.at[mine], qw_ref, sems.at[3 * shards]))
    copies.append(pltpu.make_async_copy(key_weight_ref.at[mine], kw_ref, sems.at[3 * shards + 1]))
    for copy in copies:
        copy.start()
    keys_ref[:WINDOW] = jnp.zeros((WINDOW, width), bf16)
    values_ref[:WINDOW] = jnp.zeros((WINDOW, width), bf16)
    for copy in copies:
        copy.wait()
    keys, values = keys_ref[WINDOW:], values_ref[WINDOW:]
    ext_keys, ext_values = keys_ref[:tokens], values_ref[:tokens]
    values_t, ext_keys_t, ext_aug_t, ext_aug, pair_sum = shared_parts(
        keys, values, ext_keys, ext_values, 2 * qw_ref.shape[0]
    )
    block = 256 if tokens % 256 == 0 else 128
    loss, grad_q, grad_k = head_pass(
        queries_ref[...], keys, values, ext_keys, ext_values, ext_keys_t, values_t, ext_aug_t, ext_aug, pair_sum,
        qw_ref[...], kw_ref[...], block, tokens,
    )
    half = qw_ref.shape[0]
    grads_ref[:half] = grad_q
    grads_ref[half:] = grad_k
    loss_ref[...] = jnp.broadcast_to(loss / tokens, loss_ref.shape)


def join_kernel(own_ref, other_ref, loss_a_ref, loss_b_ref, grad_q_ref, grad_k_ref, loss_ref):
    half = grad_q_ref.shape[1]
    odd = lax.rem(lax.axis_index("seq"), 2) == 1
    own, other = own_ref[...], other_ref[...]
    first, second = jnp.where(odd, other, own), jnp.where(odd, own, other)
    grad_q_ref[0], grad_q_ref[1] = first[:half], second[:half]
    grad_k_ref[0], grad_k_ref[1] = first[half:], second[half:]
    loss_ref[...] = loss_a_ref[...] + loss_b_ref[...]


def local_gathered(queries, keys, values, query_weight, key_weight):
    rows, local_heads, width = queries.shape
    features = query_weight.shape[1]
    shards, columns = lax.axis_size("seq"), lax.axis_size("head")
    tokens = rows * shards
    vmem = pl.BlockSpec(memory_space=pltpu.VMEM)
    anywhere = pl.BlockSpec(memory_space=pl.ANY)
    shape = jax.ShapeDtypeStruct
    same, other = pl.pallas_call(
        pack_kernel,
        out_shape=(shape((3 * rows, width), bf16),) * 2,
        in_specs=[vmem] * 3,
        out_specs=(vmem,) * 2,
        name="pack",
    )(queries, keys, values)
    turn = lambda x, axis, size, d: lax.ppermute(x, axis, [(i, (i + d) % size) for i in range(size)])
    pieces = [same] + [turn(other if d % 2 else same, "seq", shards, d) for d in range(1, shards)]
    grads, loss = pl.pallas_call(
        functools.partial(main_kernel, shards, rows),
        out_shape=(shape((2 * features, width), f32), shape((8, 128), f32)),
        in_specs=[anywhere] * (shards + 2),
        out_specs=(vmem,) * 2,
        scratch_shapes=[
            pltpu.VMEM((tokens + WINDOW, width), bf16),
            pltpu.VMEM((tokens + WINDOW, width), bf16),
            pltpu.VMEM((tokens, width), bf16),
            pltpu.VMEM((features, width), f32),
            pltpu.VMEM((features, width), f32),
            pltpu.SemaphoreType.DMA((3 * shards + 2,)),
        ],
        compiler_params=pltpu.CompilerParams(vmem_limit_bytes=48 << 20),
        name="main",
    )(*pieces, query_weight, key_weight)
    swap = lambda x: lax.ppermute(x, "seq", [(i, i ^ 1) for i in range(shards)])
    loss = sum((turn(loss, "head", columns, d) for d in range(1, columns)), loss)
    other_grads = swap(grads)
    other_loss = swap(loss)
    grad_query, grad_key, loss = pl.pallas_call(
        join_kernel,
        out_shape=(shape((local_heads, features, width), f32),) * 2 + (shape((8, 128), f32),),
        in_specs=[vmem] * 4,
        out_specs=(vmem,) * 3,
        name="join",
    )(grads, other_grads, loss, other_loss)
    return loss[0, :1], grad_query, grad_key


def local(queries, keys, values, query_weight, key_weight):
    rows, local_heads, width = queries.shape
    shards = lax.axis_size("seq")
    fits = shards <= LIMIT and shards % 2 == 0 and local_heads == 2 and rows == width == 128
    if fits and 2 * query_weight.shape[1] == width:
        return local_gathered(queries, keys, values, query_weight, key_weight)
    return local_general(queries, keys, values, query_weight, key_weight)


def solution(mesh):
    in_specs = (
        P(("rep", "seq"), "head", None),
        P(("rep", "seq"), None),
        P(("rep", "seq"), None),
        P(("rep", "head"), None, None),
        P(("rep", "head"), None, None),
    )
    out_specs = (P("rep"), P(("rep", "head"), None, None), P(("rep", "head"), None, None))
    return jax.shard_map(local, mesh=mesh, in_specs=in_specs, out_specs=out_specs, check_vma=False)
```

```python
import functools

import jax
import jax.numpy as jnp
from jax import lax
from jax.experimental import pallas as pl
from jax.experimental.pallas import tpu as pltpu
from jax.sharding import PartitionSpec as P

WINDOW = 64


very_low = -1e30
exact = lax.Precision.HIGHEST
f32, bf16 = jnp.float32, jnp.bfloat16
PAD = 16
LIMIT = 8
SMALL, LARGE = 4 << 20, 24 << 20


def shifted(value, axis, steps):
    count = lax.axis_size(axis)
    leading, last = (max(0, -steps), min(count, count - steps))
    return lax.ppermute(value, axis, [(source, source + steps) for source in range(leading, last)])


def prefix_2(x, axis, combine, identity):
    peers, place = (lax.axis_size(axis), lax.axis_index(axis))
    everything = jax.tree.map(lambda part: lax.all_gather(part, axis), x)
    start = jax.tree.map(
        lambda part, zero: jnp.broadcast_to(jnp.asarray(zero, part.dtype), part.shape), x, identity
    )

    def lap(k, before):
        at = peers - 1 - k
        reached = at > place
        new = combine(before, jax.tree.map(lambda part: part[at], everything))
        return jax.tree.map(lambda a, b: jnp.where(reached, a, b), new, before)

    return lax.fori_loop(0, peers, lap, start)


def feature_map(act):
    first = jnp.exp(act)
    second = jnp.exp(-act)
    return jnp.concatenate(
        [
            first / jnp.sum(first, axis=-1, keepdims=True),
            second / jnp.sum(second, axis=-1, keepdims=True),
        ],
        axis=-1,
    )


def feature_back(features, grad):
    half = features.shape[-1] // 2
    first = features[..., :half]
    second = features[..., half:]
    grad_first = grad[..., :half]
    grad_second = grad[..., half:]
    return first * (grad_first - jnp.sum(first * grad_first, axis=-1, keepdims=True)) - second * (
        grad_second - jnp.sum(second * grad_second, axis=-1, keepdims=True)
    )


def key_feature_map(keys_wide, key_weight):
    return feature_map(jnp.einsum("jd,hfd->hjf", keys_wide, key_weight, precision=exact))


def add_pair(earlier, later):
    return (earlier[0] + later[0], earlier[1] + later[1])


def flash_update(carry, queries, keys, values, query_place, key_place):
    best, total, accum = carry
    scale = queries.shape[-1] ** (-0.5)
    scores = jnp.einsum("thd,jd->htj", queries, keys, preferred_element_type=jnp.float32) * scale
    allowed = (key_place[None, :] <= query_place[:, None])[None]
    scores = jnp.where(allowed, scores, very_low)
    fresh = jnp.maximum(best, jnp.max(scores, axis=-1))
    weights = jnp.where(allowed, jnp.exp(scores - fresh[..., None]), 0.0)
    total = jnp.sum(weights, axis=-1)
    accum = jnp.einsum(
        "htj,jd->htd", weights.astype(jnp.bfloat16), values, preferred_element_type=jnp.float32
    )
    return (fresh, total, accum)


def state_update(state, keys, values, key_place, bound, key_weight):

    def accumulate(inner):
        keep = (key_place < bound).astype(jnp.float32)
        features = key_feature_map(keys.astype(jnp.float32), key_weight) * keep[None, :, None]
        return (
            jnp.einsum("hjf,jd->hfd", features, values.astype(jnp.float32), precision=exact),
            jnp.sum(features, axis=1),
        )

    return lax.cond(jnp.min(key_place) < bound, accumulate, lambda inner: inner, state)


def local_general(queries, keys, values, query_weight, key_weight):
    rows, local_heads, width = queries.shape
    shards = lax.axis_size("seq")
    device = lax.axis_index("seq")
    feature_count = 2 * query_weight.shape[1]
    total_tokens = rows * shards
    first_place = device * rows
    bound = first_place - WINDOW
    natural_place = first_place + jnp.arange(rows, dtype=jnp.int32)
    flash_init = (
        jnp.full((local_heads, rows), very_low, jnp.float32),
        jnp.zeros((local_heads, rows), jnp.float32),
        jnp.zeros((local_heads, rows, width), jnp.float32),
    )
    zero_state = (
        jnp.zeros((local_heads, feature_count, width), jnp.float32),
        jnp.zeros((local_heads, feature_count), jnp.float32),
    )
    halo_keys, halo_values = shifted((keys[rows - WINDOW :], values[rows - WINDOW :]), "seq", 1)
    ext_keys = jnp.concatenate([halo_keys, keys], axis=0)
    ext_values = jnp.concatenate([halo_values, values], axis=0)
    ext_count = rows + WINDOW
    ext_place = bound + jnp.arange(ext_count, dtype=jnp.int32)
    valid = ext_place >= 0
    covered = jnp.arange(ext_count, dtype=jnp.int32) < rows
    cover_mask = (valid & covered).astype(jnp.float32)
    ext_keys_wide = ext_keys.astype(jnp.float32)
    ext_values_wide = ext_values.astype(jnp.float32)
    key_features = key_feature_map(ext_keys_wide, key_weight)
    fold_keys, fold_values = (keys, values)
    piece_keys = lax.all_gather(fold_keys, "seq", axis=0, tiled=True)
    piece_values = lax.all_gather(fold_values, "seq", axis=0, tiled=True)
    key_place = jnp.arange(piece_keys.shape[0], dtype=jnp.int32)

    def attend(inner):
        flash = flash_update(inner[0], queries, piece_keys, piece_values, natural_place, key_place)
        state = state_update(inner[1], piece_keys, piece_values, key_place, bound, key_weight)
        return (flash, state)

    flash, folded = lax.cond(
        jnp.int32(0) < first_place + rows, attend, lambda inner: inner, (flash_init, zero_state)
    )
    teacher = jnp.transpose(flash[2] / flash[1][..., None], (1, 0, 2)).astype(jnp.bfloat16)
    scale = width ** (-0.5)
    scores = (
        jnp.einsum("thd,jd->htj", queries, ext_keys, preferred_element_type=jnp.float32) * scale
    )
    window = (
        (ext_place[None, :] <= natural_place[:, None])
        & (ext_place[None, :] > natural_place[:, None] - WINDOW)
        & valid[None, :]
    )[None]
    linear_mask = ((ext_place[None, :] <= natural_place[:, None] - WINDOW) & valid[None, :])[None]
    window_best = jnp.max(jnp.where(window, scores, very_low), axis=-1)
    window_weights = jnp.where(window, jnp.exp(scores - window_best[..., None]), 0.0)
    window_total = jnp.sum(window_weights, axis=-1)
    window_sum = jnp.einsum(
        "htj,jd->htd",
        window_weights.astype(jnp.bfloat16),
        ext_values,
        preferred_element_type=jnp.float32,
    )
    queries_wide = queries.astype(jnp.float32)
    query_features = feature_map(
        jnp.einsum("thd,hfd->htf", queries_wide, query_weight, precision=exact)
    )
    linear = jnp.where(
        linear_mask, jnp.einsum("htf,hjf->htj", query_features, key_features, precision=exact), 0.0
    )
    linear_sum = jnp.einsum("htj,jd->htd", linear, ext_values_wide, precision=exact) + jnp.einsum(
        "htf,hfd->htd", query_features, folded[0], precision=exact
    )
    linear_total = jnp.sum(linear, axis=-1) + jnp.einsum(
        "htf,hf->ht", query_features, folded[1], precision=exact
    )
    lift = jnp.exp(-window_best)
    denominator = window_total + lift * linear_total
    student = (window_sum + lift[..., None] * linear_sum) / denominator[..., None]
    teacher_wide = jnp.transpose(teacher, (1, 0, 2)).astype(jnp.float32)
    difference = student - teacher_wide
    loss_part = jnp.sum(difference * difference) / total_tokens
    grad_out = 2.0 * difference / total_tokens
    num_grad = lift[..., None] * grad_out / denominator[..., None]
    den_grad = -lift * jnp.sum(grad_out * student, axis=-1) / denominator
    adjoint = (
        jnp.einsum("htf,htd->hfd", query_features, num_grad, precision=exact),
        jnp.einsum("htf,ht->hf", query_features, den_grad, precision=exact),
    )
    later = prefix_2(adjoint, "seq", add_pair, zero_state)
    link = jnp.where(
        linear_mask,
        jnp.einsum("htd,jd->htj", num_grad, ext_values_wide, precision=exact) + den_grad[..., None],
        0.0,
    )
    query_feature_grad = (
        jnp.einsum("htj,hjf->htf", link, key_features, precision=exact)
        + jnp.einsum("htd,hfd->htf", num_grad, folded[0], precision=exact)
        + den_grad[..., None] * folded[1][:, None, :]
    )
    key_feature_grad = (
        jnp.einsum("htj,htf->hjf", link, query_features, precision=exact)
        + jnp.einsum("jd,hfd->hjf", ext_values_wide, later[0], precision=exact)
        + later[1][:, None, :]
    )
    key_feature_grad = key_feature_grad * cover_mask[None, :, None]
    query_act_grad = feature_back(query_features, query_feature_grad)
    key_act_grad = feature_back(key_features, key_feature_grad)
    grad_query = jnp.einsum("htf,thd->hfd", query_act_grad, queries_wide, precision=exact)
    grad_key = jnp.einsum("hjf,jd->hfd", key_act_grad, ext_keys_wide, precision=exact)
    grad_query, grad_key = lax.psum((grad_query, grad_key), "seq")
    loss = lax.psum(loss_part, ("seq", "head")).reshape(1)
    return (loss, grad_query, grad_key)


def dot(a, b):
    return lax.dot_general(a, b, (((1,), (0,)), ((), ())), preferred_element_type=f32)


def dot_t(a, b):
    return lax.dot_general(a, b, (((1,), (1,)), ((), ())), preferred_element_type=f32)


def split(x):
    high = x.astype(bf16)
    return high, (x - high.astype(f32)).astype(bf16)


def dot3(a, b):
    return dot(a[0], b[0]) + (dot(a[0], b[1]) + dot(a[1], b[0]))


def dot_left(a, b):
    return dot(a[0], b) + dot(a[1], b)


def dot_right(a, b):
    return dot(a, b[0]) + dot(a, b[1])


def iota(shape, axis):
    return lax.broadcasted_iota(jnp.int32, shape, axis)


def forward_pass(queries, keys, ext_keys, values_t, ext_aug_t, pair_sum, query_weight, key_weight, block, tokens_total):
    tokens, width = queries.shape
    blocks = tokens // block
    scale = width ** (-0.5)
    wq = split(jnp.concatenate([query_weight, -query_weight], axis=0))
    wk = split(jnp.concatenate([key_weight, -key_weight], axis=0))
    raised_t = jnp.exp(dot_t(wq[0], queries) + dot_t(wq[1], queries))
    qf_t = raised_t / dot_right(pair_sum, split(raised_t))
    raised = jnp.exp(dot_t(ext_keys, wk[0]) + dot_t(ext_keys, wk[1]))
    kf = raised / dot_left(split(raised), pair_sum)
    kf = jnp.where(iota(kf.shape, 0) >= WINDOW, kf, 0.0)
    qf_ts, kf_s = split(qf_t), split(kf)
    tri = iota((block, block), 0) <= iota((block, block), 1)
    near = iota((block + WINDOW, block), 0) > iota((block + WINDOW, block), 1)
    loss = jnp.zeros((1, 1), f32)
    state_t = None
    nums, dens = [], []
    for b in range(blocks):
        lo, hi = b * block, (b + 1) * block
        here = (slice(None), slice(lo, hi))
        rows = (slice(lo, hi), slice(None))
        scores = dot_t(keys[:hi], queries[lo:hi]) * scale
        tail = scores[lo:]
        causal = jnp.where(tri, tail, very_low)
        best = jnp.max(causal, axis=0, keepdims=True)
        if b:
            best = jnp.maximum(best, jnp.max(scores[:lo], axis=0, keepdims=True))
        weights = jnp.where(tri, jnp.exp(tail - best), 0.0)
        total = jnp.sum(weights, axis=0, keepdims=True)
        teacher = dot(values_t[:, lo:hi], weights.astype(bf16))
        if b:
            weights = jnp.exp(scores[:lo] - best)
            total = total + jnp.sum(weights, axis=0, keepdims=True)
            teacher = teacher + dot(values_t[:, :lo], weights.astype(bf16))
        teacher = (teacher / total).astype(bf16).astype(f32)
        inside = tri & near[WINDOW:]
        wbest = jnp.max(jnp.where(inside, tail, very_low), axis=0, keepdims=True)
        if b:
            early = jnp.where(near[:WINDOW], scores[lo - WINDOW : lo], very_low)
            wbest = jnp.maximum(wbest, jnp.max(early, axis=0, keepdims=True))
        weights = jnp.where(inside, jnp.exp(tail - wbest), 0.0)
        wtotal = jnp.sum(weights, axis=0, keepdims=True)
        wsum = dot(values_t[:, lo:hi], weights.astype(bf16))
        if b:
            weights = jnp.where(near[:WINDOW], jnp.exp(early - wbest), 0.0)
            wtotal = wtotal + jnp.sum(weights, axis=0, keepdims=True)
            weights = jnp.concatenate([jnp.zeros((128 - WINDOW, block), bf16), weights.astype(bf16)], axis=0)
            wsum = wsum + dot(values_t[:, lo - 128 : lo], weights)
        linear = jnp.where(tri, dot3(cut(kf_s, rows), cut(qf_ts, here)), 0.0)
        aug = dot_right(ext_aug_t[:, lo:hi], split(linear))
        if b:
            aug = aug + dot3(split(state_t), cut(qf_ts, here))
        if b + 1 < blocks:
            grown_t = dot_right(ext_aug_t[:, lo:hi], cut(kf_s, rows))
            state_t = grown_t if state_t is None else state_t + grown_t
        lift = jnp.exp(-wbest)
        over = 1.0 / (wtotal + lift * aug[width : width + 1])
        student = (wsum + lift * aug[:width]) * over
        difference = student - teacher
        loss = loss + jnp.sum(jnp.sum(difference * difference, axis=0, keepdims=True), axis=1, keepdims=True)
        grad = difference * (2.0 / tokens_total)
        nums.append(grad * (lift * over))
        dens.append(-(lift * over) * jnp.sum(grad * student, axis=0, keepdims=True))
    return loss, qf_t, kf, nums, dens


def cut(pair, at):
    return tuple(part[at] for part in pair)


def backward_pass(qf_t, kf, nums, dens, queries, ext_values, ext_keys_t, pair_sum, block):
    width, tokens = queries.shape[1], queries.shape[0]
    blocks = tokens // block
    tri = iota((block, block), 0) <= iota((block, block), 1)
    qf_s, kf_ts = split(qf_t.T), split(kf.T)
    ext_aug = jnp.concatenate([ext_values, (iota((tokens, width), 1) == 0).astype(bf16)], axis=1)
    states = [None]
    for b in range(blocks - 1):
        lo, hi = b * block, (b + 1) * block
        grown = dot_left(cut(kf_ts, (slice(None), slice(lo, hi))), ext_aug[lo:hi])
        states.append(grown if b == 0 else states[-1] + grown)
    grad_q = jnp.zeros((qf_t.shape[0], width), f32)
    grad_k = jnp.zeros((width, kf.shape[1]), f32)
    later = None
    for b in reversed(range(blocks)):
        lo, hi = b * block, (b + 1) * block
        here = (slice(None), slice(lo, hi))
        rows = (slice(lo, hi), slice(None))
        num, den = nums[b], dens[b]
        num_s = split(num)
        link = jnp.where(tri, dot_right(ext_values[lo:hi], num_s) + den, 0.0)
        link_s = split(link)
        qfg = dot3(cut(kf_ts, here), link_s)
        if b:
            qfg = qfg + dot3(split(states[b][:, :width]), num_s) + states[b][:, width : width + 1] * den
        kfg = dot3(link_s, cut(qf_s, rows))
        if later is not None:
            kfg = kfg + dot_right(ext_values[lo:hi], split(later[:width])) + later[width : width + 1]
        if b:
            fill = jnp.concatenate([num, den, jnp.zeros((PAD - 1, block), f32)], axis=0)
            grown = dot3(split(fill), cut(qf_s, rows))
            later = grown if later is None else later + grown
        f_t = qf_t[here]
        back = f_t * (qfg - dot_right(pair_sum, split(f_t * qfg)))
        grad_q = grad_q + dot_left(split(back), queries[lo:hi])
        f = kf[rows]
        back = f * (kfg - dot_left(split(f * kfg), pair_sum))
        grad_k = grad_k + dot_right(ext_keys_t[:, lo:hi], split(back))
    half = grad_q.shape[0] // 2
    grad_k = grad_k.T
    return grad_q[:half] - grad_q[half:], grad_k[:half] - grad_k[half:]


def turned(x):
    eye = (iota((x.shape[1], x.shape[1]), 0) == iota((x.shape[1], x.shape[1]), 1)).astype(bf16)
    return dot_t(eye, x).astype(bf16)


def with_ones(x_t):
    return jnp.concatenate([x_t, (iota((PAD, x_t.shape[1]), 0) == 0).astype(bf16)], axis=0)


def pair_sums(features):
    half = features // 2
    return ((iota((features, features), 0) < half) == (iota((features, features), 1) < half)).astype(bf16)


def pack_kernel(queries_ref, keys_ref, values_ref, same_ref, other_ref, queries_in, sems):
    rows = keys_ref.shape[0]
    copies = [
        pltpu.make_async_copy(queries_ref, queries_in, sems.at[0]),
        pltpu.make_async_copy(keys_ref, same_ref.at[pl.ds(0, rows)], sems.at[1]),
        pltpu.make_async_copy(values_ref, same_ref.at[pl.ds(rows, rows)], sems.at[2]),
        pltpu.make_async_copy(keys_ref, other_ref.at[pl.ds(0, rows)], sems.at[3]),
        pltpu.make_async_copy(values_ref, other_ref.at[pl.ds(rows, rows)], sems.at[4]),
    ]
    for copy in copies:
        copy.start()
    odd = lax.rem(lax.axis_index("seq"), 2) == 1
    copies[0].wait()
    first, second = queries_in[:, 0, :], queries_in[:, 1, :]
    same_ref[2 * rows :] = jnp.where(odd, second, first)
    other_ref[2 * rows :] = jnp.where(odd, first, second)
    for copy in copies[1:]:
        copy.wait()


def forward_kernel(shards, rows, *refs):
    blocks_in = refs[:shards]
    query_weight_ref, key_weight_ref, loss_ref, keys_ref, values_ref, queries_ref, qf_ref, kf_ref, num_ref, den_ref = refs[shards : shards + 10]
    qw_ref, kw_ref, sems = refs[shards + 10 :]
    tokens, width = queries_ref.shape
    place = lax.axis_index("seq")
    mine = lax.rem(place, 2)
    copies = []
    for d in range(shards):
        source = lax.rem(place + shards - d, shards)
        at = pl.multiple_of(source * rows, rows)
        for k, (ref, offset) in enumerate(((keys_ref, WINDOW), (values_ref, WINDOW), (queries_ref, 0))):
            copies.append(
                pltpu.make_async_copy(
                    blocks_in[d].at[pl.ds(k * rows, rows)], ref.at[pl.ds(at + offset, rows)], sems.at[3 * d + k]
                )
            )
    copies.append(pltpu.make_async_copy(query_weight_ref.at[mine], qw_ref, sems.at[3 * shards]))
    copies.append(pltpu.make_async_copy(key_weight_ref.at[mine], kw_ref, sems.at[3 * shards + 1]))
    for copy in copies:
        copy.start()
    keys_ref[:WINDOW] = jnp.zeros((WINDOW, width), bf16)
    values_ref[:WINDOW] = jnp.zeros((WINDOW, width), bf16)
    for copy in copies:
        copy.wait()
    block = block_of(tokens)
    loss, qf_t, kf, nums, dens = forward_pass(
        queries_ref[...], keys_ref[WINDOW:], keys_ref[:tokens], turned(values_ref[WINDOW:]),
        with_ones(turned(values_ref[:tokens])), pair_sums(2 * qw_ref.shape[0]), qw_ref[...], kw_ref[...], block, tokens,
    )
    qf_ref[...] = qf_t
    kf_ref[...] = kf
    for b in range(tokens // block):
        at = slice(b * block, (b + 1) * block)
        num_ref[:, at] = nums[b]
        den_ref[:, at] = jnp.broadcast_to(dens[b], (8, block))
    loss_ref[...] = jnp.broadcast_to(loss / tokens, loss_ref.shape)


def block_of(tokens):
    return 256 if tokens % 256 == 0 else 128


def backward_kernel(keys_ref, values_ref, queries_ref, qf_ref, kf_ref, num_ref, den_ref, grads_ref):
    tokens = queries_ref.shape[0]
    half = qf_ref.shape[0] // 2
    block = block_of(tokens)
    cuts = [slice(b * block, (b + 1) * block) for b in range(tokens // block)]
    grads_ref[:half], grads_ref[half:] = backward_pass(
        qf_ref[...], kf_ref[...], [num_ref[:, at] for at in cuts], [den_ref[:1, at] for at in cuts],
        queries_ref[...], values_ref[:tokens], turned(keys_ref[:tokens]), pair_sums(2 * half), block,
    )


def join_kernel(own_ref, other_ref, *refs):
    loss_refs = refs[:-3]
    grad_q_ref, grad_k_ref, loss_ref = refs[-3:]
    half = grad_q_ref.shape[1]
    odd = lax.rem(lax.axis_index("seq"), 2) == 1
    own, other = own_ref[...], other_ref[...]
    first, second = jnp.where(odd, other, own), jnp.where(odd, own, other)
    grad_q_ref[0], grad_q_ref[1] = first[:half], second[:half]
    grad_k_ref[0], grad_k_ref[1] = first[half:], second[half:]
    loss_ref[0] = sum(ref[0, 0] for ref in loss_refs)


def local_gathered(queries, keys, values, query_weight, key_weight):
    rows, local_heads, width = queries.shape
    features = query_weight.shape[1]
    shards, columns = lax.axis_size("seq"), lax.axis_size("head")
    tokens = rows * shards
    vmem = pl.BlockSpec(memory_space=pltpu.VMEM)
    anywhere = pl.BlockSpec(memory_space=pl.ANY)
    shape = jax.ShapeDtypeStruct
    same, other = pl.pallas_call(
        pack_kernel,
        out_shape=(shape((3 * rows, width), bf16),) * 2,
        in_specs=[pl.BlockSpec(memory_space=pltpu.HBM)] * 3,
        out_specs=(vmem,) * 2,
        scratch_shapes=[pltpu.VMEM(queries.shape, bf16), pltpu.SemaphoreType.DMA((5,))],
        compiler_params=pltpu.CompilerParams(vmem_limit_bytes=SMALL),
        name="pack",
    )(*(pltpu.with_memory_space_constraint(x, pltpu.HBM) for x in (queries, keys, values)))
    turn = lambda x, axis, size, d: lax.ppermute(x, axis, [(i, (i + d) % size) for i in range(size)])
    pieces = [same] + [turn(other if d % 2 else same, "seq", shards, d) for d in range(1, shards)]
    loss, *kept = pl.pallas_call(
        functools.partial(forward_kernel, shards, rows),
        out_shape=(
            shape((8, 128), f32),
            shape((tokens + WINDOW, width), bf16),
            shape((tokens + WINDOW, width), bf16),
            shape((tokens, width), bf16),
            shape((2 * features, tokens), f32),
            shape((tokens, 2 * features), f32),
            shape((width, tokens), f32),
            shape((8, tokens), f32),
        ),
        in_specs=[anywhere] * (shards + 2),
        out_specs=(vmem,) * 8,
        scratch_shapes=[
            pltpu.VMEM((features, width), f32),
            pltpu.VMEM((features, width), f32),
            pltpu.SemaphoreType.DMA((3 * shards + 2,)),
        ],
        compiler_params=pltpu.CompilerParams(vmem_limit_bytes=LARGE),
        cost_estimate=pl.CostEstimate(flops=10**9, bytes_accessed=10**7, transcendentals=10**6),
        name="forward",
    )(*pieces, query_weight, key_weight)
    swap = lambda x: lax.ppermute(x, "seq", [(i, i ^ 1) for i in range(shards)])
    loss = sum((turn(loss, "head", columns, d) for d in range(1, columns)), loss)
    grads = pl.pallas_call(
        backward_kernel,
        out_shape=shape((2 * features, width), f32),
        in_specs=[vmem] * 7,
        out_specs=vmem,
        compiler_params=pltpu.CompilerParams(vmem_limit_bytes=LARGE),
        cost_estimate=pl.CostEstimate(flops=10**9, bytes_accessed=10**7, transcendentals=10**6),
        name="backward",
    )(*kept)
    other_grads = swap(grads)
    losses = [loss, swap(loss)]
    grad_query, grad_key, loss = pl.pallas_call(
        join_kernel,
        out_shape=(shape((local_heads, features, width), f32),) * 2 + (shape((1,), f32),),
        in_specs=[vmem] * 4,
        out_specs=(vmem, vmem, pl.BlockSpec(memory_space=pltpu.SMEM)),
        compiler_params=pltpu.CompilerParams(vmem_limit_bytes=SMALL),
        name="join",
    )(grads, other_grads, *losses)
    return loss, grad_query, grad_key


def local(queries, keys, values, query_weight, key_weight):
    rows, local_heads, width = queries.shape
    shards = lax.axis_size("seq")
    fits = shards <= LIMIT and shards % 2 == 0 and local_heads == 2 and rows == width == 128
    if fits and 2 * query_weight.shape[1] == width:
        return local_gathered(queries, keys, values, query_weight, key_weight)
    return local_general(queries, keys, values, query_weight, key_weight)


def solution(mesh):
    in_specs = (
        P(("rep", "seq"), "head", None),
        P(("rep", "seq"), None),
        P(("rep", "seq"), None),
        P(("rep", "head"), None, None),
        P(("rep", "head"), None, None),
    )
    out_specs = (P("rep"), P(("rep", "head"), None, None), P(("rep", "head"), None, None))
    return jax.shard_map(local, mesh=mesh, in_specs=in_specs, out_specs=out_specs, check_vma=False)
```

```python
import functools

import jax
import jax.numpy as jnp
from jax import lax
from jax.experimental import pallas as pl
from jax.experimental.pallas import tpu as pltpu
from jax.sharding import PartitionSpec as P

WINDOW = 64


very_low = -1e30
exact = lax.Precision.HIGHEST
f32, bf16 = jnp.float32, jnp.bfloat16
PAD = 16
SMALL, LARGE = 4 << 20, 24 << 20


def shifted(value, axis, steps):
    count = lax.axis_size(axis)
    leading, last = (max(0, -steps), min(count, count - steps))
    return lax.ppermute(value, axis, [(source, source + steps) for source in range(leading, last)])


def prefix_2(x, axis, combine, identity):
    peers, place = (lax.axis_size(axis), lax.axis_index(axis))
    everything = jax.tree.map(lambda part: lax.all_gather(part, axis), x)
    start = jax.tree.map(
        lambda part, zero: jnp.broadcast_to(jnp.asarray(zero, part.dtype), part.shape), x, identity
    )

    def lap(k, before):
        at = peers - 1 - k
        reached = at > place
        new = combine(before, jax.tree.map(lambda part: part[at], everything))
        return jax.tree.map(lambda a, b: jnp.where(reached, a, b), new, before)

    return lax.fori_loop(0, peers, lap, start)


def feature_map(act):
    first = jnp.exp(act)
    second = jnp.exp(-act)
    return jnp.concatenate(
        [
            first / jnp.sum(first, axis=-1, keepdims=True),
            second / jnp.sum(second, axis=-1, keepdims=True),
        ],
        axis=-1,
    )


def feature_back(features, grad):
    half = features.shape[-1] // 2
    first = features[..., :half]
    second = features[..., half:]
    grad_first = grad[..., :half]
    grad_second = grad[..., half:]
    return first * (grad_first - jnp.sum(first * grad_first, axis=-1, keepdims=True)) - second * (
        grad_second - jnp.sum(second * grad_second, axis=-1, keepdims=True)
    )


def key_feature_map(keys_wide, key_weight):
    return feature_map(jnp.einsum("jd,hfd->hjf", keys_wide, key_weight, precision=exact))


def add_pair(earlier, later):
    return (earlier[0] + later[0], earlier[1] + later[1])


def flash_update(carry, queries, keys, values, query_place, key_place):
    best, total, accum = carry
    scale = queries.shape[-1] ** (-0.5)
    scores = jnp.einsum("thd,jd->htj", queries, keys, preferred_element_type=jnp.float32) * scale
    allowed = (key_place[None, :] <= query_place[:, None])[None]
    scores = jnp.where(allowed, scores, very_low)
    fresh = jnp.maximum(best, jnp.max(scores, axis=-1))
    weights = jnp.where(allowed, jnp.exp(scores - fresh[..., None]), 0.0)
    total = jnp.sum(weights, axis=-1)
    accum = jnp.einsum(
        "htj,jd->htd", weights.astype(jnp.bfloat16), values, preferred_element_type=jnp.float32
    )
    return (fresh, total, accum)


def state_update(state, keys, values, key_place, bound, key_weight):

    def accumulate(inner):
        keep = (key_place < bound).astype(jnp.float32)
        features = key_feature_map(keys.astype(jnp.float32), key_weight) * keep[None, :, None]
        return (
            jnp.einsum("hjf,jd->hfd", features, values.astype(jnp.float32), precision=exact),
            jnp.sum(features, axis=1),
        )

    return lax.cond(jnp.min(key_place) < bound, accumulate, lambda inner: inner, state)


def local_general(queries, keys, values, query_weight, key_weight):
    rows, local_heads, width = queries.shape
    shards = lax.axis_size("seq")
    device = lax.axis_index("seq")
    feature_count = 2 * query_weight.shape[1]
    total_tokens = rows * shards
    first_place = device * rows
    bound = first_place - WINDOW
    natural_place = first_place + jnp.arange(rows, dtype=jnp.int32)
    flash_init = (
        jnp.full((local_heads, rows), very_low, jnp.float32),
        jnp.zeros((local_heads, rows), jnp.float32),
        jnp.zeros((local_heads, rows, width), jnp.float32),
    )
    zero_state = (
        jnp.zeros((local_heads, feature_count, width), jnp.float32),
        jnp.zeros((local_heads, feature_count), jnp.float32),
    )
    halo_keys, halo_values = shifted((keys[rows - WINDOW :], values[rows - WINDOW :]), "seq", 1)
    ext_keys = jnp.concatenate([halo_keys, keys], axis=0)
    ext_values = jnp.concatenate([halo_values, values], axis=0)
    ext_count = rows + WINDOW
    ext_place = bound + jnp.arange(ext_count, dtype=jnp.int32)
    valid = ext_place >= 0
    covered = jnp.arange(ext_count, dtype=jnp.int32) < rows
    cover_mask = (valid & covered).astype(jnp.float32)
    ext_keys_wide = ext_keys.astype(jnp.float32)
    ext_values_wide = ext_values.astype(jnp.float32)
    key_features = key_feature_map(ext_keys_wide, key_weight)
    fold_keys, fold_values = (keys, values)
    piece_keys = lax.all_gather(fold_keys, "seq", axis=0, tiled=True)
    piece_values = lax.all_gather(fold_values, "seq", axis=0, tiled=True)
    key_place = jnp.arange(piece_keys.shape[0], dtype=jnp.int32)

    def attend(inner):
        flash = flash_update(inner[0], queries, piece_keys, piece_values, natural_place, key_place)
        state = state_update(inner[1], piece_keys, piece_values, key_place, bound, key_weight)
        return (flash, state)

    flash, folded = lax.cond(
        jnp.int32(0) < first_place + rows, attend, lambda inner: inner, (flash_init, zero_state)
    )
    teacher = jnp.transpose(flash[2] / flash[1][..., None], (1, 0, 2)).astype(jnp.bfloat16)
    scale = width ** (-0.5)
    scores = (
        jnp.einsum("thd,jd->htj", queries, ext_keys, preferred_element_type=jnp.float32) * scale
    )
    window = (
        (ext_place[None, :] <= natural_place[:, None])
        & (ext_place[None, :] > natural_place[:, None] - WINDOW)
        & valid[None, :]
    )[None]
    linear_mask = ((ext_place[None, :] <= natural_place[:, None] - WINDOW) & valid[None, :])[None]
    window_best = jnp.max(jnp.where(window, scores, very_low), axis=-1)
    window_weights = jnp.where(window, jnp.exp(scores - window_best[..., None]), 0.0)
    window_total = jnp.sum(window_weights, axis=-1)
    window_sum = jnp.einsum(
        "htj,jd->htd",
        window_weights.astype(jnp.bfloat16),
        ext_values,
        preferred_element_type=jnp.float32,
    )
    queries_wide = queries.astype(jnp.float32)
    query_features = feature_map(
        jnp.einsum("thd,hfd->htf", queries_wide, query_weight, precision=exact)
    )
    linear = jnp.where(
        linear_mask, jnp.einsum("htf,hjf->htj", query_features, key_features, precision=exact), 0.0
    )
    linear_sum = jnp.einsum("htj,jd->htd", linear, ext_values_wide, precision=exact) + jnp.einsum(
        "htf,hfd->htd", query_features, folded[0], precision=exact
    )
    linear_total = jnp.sum(linear, axis=-1) + jnp.einsum(
        "htf,hf->ht", query_features, folded[1], precision=exact
    )
    lift = jnp.exp(-window_best)
    denominator = window_total + lift * linear_total
    student = (window_sum + lift[..., None] * linear_sum) / denominator[..., None]
    teacher_wide = jnp.transpose(teacher, (1, 0, 2)).astype(jnp.float32)
    difference = student - teacher_wide
    loss_part = jnp.sum(difference * difference) / total_tokens
    grad_out = 2.0 * difference / total_tokens
    num_grad = lift[..., None] * grad_out / denominator[..., None]
    den_grad = -lift * jnp.sum(grad_out * student, axis=-1) / denominator
    adjoint = (
        jnp.einsum("htf,htd->hfd", query_features, num_grad, precision=exact),
        jnp.einsum("htf,ht->hf", query_features, den_grad, precision=exact),
    )
    later = prefix_2(adjoint, "seq", add_pair, zero_state)
    link = jnp.where(
        linear_mask,
        jnp.einsum("htd,jd->htj", num_grad, ext_values_wide, precision=exact) + den_grad[..., None],
        0.0,
    )
    query_feature_grad = (
        jnp.einsum("htj,hjf->htf", link, key_features, precision=exact)
        + jnp.einsum("htd,hfd->htf", num_grad, folded[0], precision=exact)
        + den_grad[..., None] * folded[1][:, None, :]
    )
    key_feature_grad = (
        jnp.einsum("htj,htf->hjf", link, query_features, precision=exact)
        + jnp.einsum("jd,hfd->hjf", ext_values_wide, later[0], precision=exact)
        + later[1][:, None, :]
    )
    key_feature_grad = key_feature_grad * cover_mask[None, :, None]
    query_act_grad = feature_back(query_features, query_feature_grad)
    key_act_grad = feature_back(key_features, key_feature_grad)
    grad_query = jnp.einsum("htf,thd->hfd", query_act_grad, queries_wide, precision=exact)
    grad_key = jnp.einsum("hjf,jd->hfd", key_act_grad, ext_keys_wide, precision=exact)
    grad_query, grad_key = lax.psum((grad_query, grad_key), "seq")
    loss = lax.psum(loss_part, ("seq", "head")).reshape(1)
    return (loss, grad_query, grad_key)


def dot(a, b):
    return lax.dot_general(a, b, (((1,), (0,)), ((), ())), preferred_element_type=f32)


def dot_t(a, b):
    return lax.dot_general(a, b, (((1,), (1,)), ((), ())), preferred_element_type=f32)


def split(x):
    high = x.astype(bf16)
    return high, (x - high.astype(f32)).astype(bf16)


def dot3(a, b):
    return dot(jnp.concatenate([a[0], a[1], a[0]], axis=1), jnp.concatenate([b[0], b[0], b[1]], axis=0))


def dot_left(a, b):
    return dot(jnp.concatenate(a, axis=1), jnp.concatenate([b, b], axis=0))


def dot_right(a, b):
    return dot(jnp.concatenate([a, a], axis=1), jnp.concatenate(b, axis=0))


def iota(shape, axis):
    return lax.broadcasted_iota(jnp.int32, shape, axis)


def feature_weights(weights):
    high, low = split(jnp.concatenate([part for weight in weights for part in (weight, -weight)], axis=0))
    return jnp.concatenate([high, low], axis=1)


def features_of(rows, weights):
    raised = jnp.exp(dot_t(jnp.concatenate([rows, rows], axis=1), weights))
    size, half = raised.shape[1], rows.shape[1] // 2
    same = (iota((size, size), 0) // half == iota((size, size), 1) // half).astype(bf16)
    return raised / dot_left(split(raised), same)


def absorb(piece_rows, source, kv, q, query_weight_ref, key_weight_ref, buffers):
    keys_ref, values_ref, queries_ref, kf_ref, qn_ref, qt_ref = buffers
    heads, width = queries_ref.shape[0], queries_ref.shape[2]
    at = pl.multiple_of(source * piece_rows, piece_rows)
    here, shifted = pl.ds(at, piece_rows), pl.ds(pl.multiple_of(at + WINDOW, WINDOW), piece_rows)
    if kv is not None:
        ref, skip = kv
        keys = ref[skip * piece_rows : (skip + 1) * piece_rows]
        keys_ref[shifted] = keys
        values_ref[shifted] = ref[(skip + 1) * piece_rows : (skip + 2) * piece_rows]
        found = features_of(keys, feature_weights([key_weight_ref[h] for h in range(heads)]))
        for h in range(heads):
            high, low = split(found[:, h * width : (h + 1) * width])
            kf_ref[h, shifted, :width] = high
            kf_ref[h, shifted, width:] = low
    if q is not None:
        ref, skip = q
        for h in range(heads):
            queries = ref[(skip + h) * piece_rows : (skip + h + 1) * piece_rows]
            queries_ref[h, here] = queries
            found = features_of(queries, feature_weights([query_weight_ref[h]]))
            high, low = split(found)
            qn_ref[h, here, :width] = high
            qn_ref[h, here, width:] = low
            high, low = split(found.T)
            qt_ref[h, :width, here] = high
            qt_ref[h, width:, here] = low


def forward_pass(queries, keys, kf_s, qf_ts, values_t, ext_aug_t, block, tokens_total):
    tokens, width = queries.shape
    blocks = tokens // block
    scale = width ** (-0.5)
    tri = iota((block, block), 0) <= iota((block, block), 1)
    near = iota((block + WINDOW, block), 0) > iota((block + WINDOW, block), 1)
    loss = jnp.zeros((1, 1), f32)
    state_t = None
    nums, dens = [], []
    for b in range(blocks):
        lo, hi = b * block, (b + 1) * block
        here = (slice(None), slice(lo, hi))
        rows = (slice(lo, hi), slice(None))
        scores = dot_t(keys[:hi], queries[lo:hi]) * scale
        tail = scores[lo:]
        causal = jnp.where(tri, tail, very_low)
        best = jnp.max(causal, axis=0, keepdims=True)
        if b:
            best = jnp.maximum(best, jnp.max(scores[:lo], axis=0, keepdims=True))
        weights = jnp.where(tri, jnp.exp(tail - best), 0.0)
        total = jnp.sum(weights, axis=0, keepdims=True)
        teacher = dot(values_t[:, lo:hi], weights.astype(bf16))
        if b:
            weights = jnp.exp(scores[:lo] - best)
            total = total + jnp.sum(weights, axis=0, keepdims=True)
            teacher = teacher + dot(values_t[:, :lo], weights.astype(bf16))
        teacher = (teacher / total).astype(bf16).astype(f32)
        inside = tri & near[WINDOW:]
        wbest = jnp.max(jnp.where(inside, tail, very_low), axis=0, keepdims=True)
        if b:
            early = jnp.where(near[:WINDOW], scores[lo - WINDOW : lo], very_low)
            wbest = jnp.maximum(wbest, jnp.max(early, axis=0, keepdims=True))
        weights = jnp.where(inside, jnp.exp(tail - wbest), 0.0)
        wtotal = jnp.sum(weights, axis=0, keepdims=True)
        wsum = dot(values_t[:, lo:hi], weights.astype(bf16))
        if b:
            weights = jnp.where(near[:WINDOW], jnp.exp(early - wbest), 0.0)
            wtotal = wtotal + jnp.sum(weights, axis=0, keepdims=True)
            weights = jnp.concatenate([jnp.zeros((128 - WINDOW, block), bf16), weights.astype(bf16)], axis=0)
            wsum = wsum + dot(values_t[:, lo - 128 : lo], weights)
        linear = jnp.where(tri, dot3(cut(kf_s, rows), cut(qf_ts, here)), 0.0)
        aug = dot_right(ext_aug_t[:, lo:hi], split(linear))
        if b:
            aug = aug + dot3(split(state_t), cut(qf_ts, here))
        if b + 1 < blocks:
            grown_t = dot_right(ext_aug_t[:, lo:hi], cut(kf_s, rows))
            state_t = grown_t if state_t is None else state_t + grown_t
        lift = jnp.exp(-wbest)
        over = 1.0 / (wtotal + lift * aug[width : width + 1])
        student = (wsum + lift * aug[:width]) * over
        difference = student - teacher
        loss = loss + jnp.sum(jnp.sum(difference * difference, axis=0, keepdims=True), axis=1, keepdims=True)
        grad = difference * (2.0 / tokens_total)
        nums.append(grad * (lift * over))
        dens.append(-(lift * over) * jnp.sum(grad * student, axis=0, keepdims=True))
    return loss, nums, dens


def cut(pair, at):
    return tuple(part[at] for part in pair)


def backward_pass(kf_s, qf_s, qf_ts, nums, dens, queries, ext_values, ext_keys_t, pair_sum, block):
    width, tokens = queries.shape[1], queries.shape[0]
    blocks = tokens // block
    tri = iota((block, block), 0) <= iota((block, block), 1)
    kf, qf_t = joined(kf_s), joined(qf_ts)
    kf_ts = split(kf.T)
    ext_aug = jnp.concatenate([ext_values, (iota((tokens, width), 1) == 0).astype(bf16)], axis=1)
    states = [None]
    for b in range(blocks - 1):
        lo, hi = b * block, (b + 1) * block
        grown = dot_left(cut(kf_ts, (slice(None), slice(lo, hi))), ext_aug[lo:hi])
        states.append(grown if b == 0 else states[-1] + grown)
    grad_q = jnp.zeros((qf_t.shape[0], width), f32)
    grad_k = jnp.zeros((width, kf.shape[1]), f32)
    later = None
    for b in reversed(range(blocks)):
        lo, hi = b * block, (b + 1) * block
        here = (slice(None), slice(lo, hi))
        rows = (slice(lo, hi), slice(None))
        num, den = nums[b], dens[b]
        num_s = split(num)
        link = jnp.where(tri, dot_right(ext_values[lo:hi], num_s) + den, 0.0)
        link_s = split(link)
        qfg = dot3(cut(kf_ts, here), link_s)
        if b:
            qfg = qfg + dot3(split(states[b][:, :width]), num_s) + states[b][:, width : width + 1] * den
        kfg = dot3(link_s, cut(qf_s, rows))
        if later is not None:
            kfg = kfg + dot_right(ext_values[lo:hi], split(later[:width])) + later[width : width + 1]
        if b:
            fill = jnp.concatenate([num, den, jnp.zeros((PAD - 1, block), f32)], axis=0)
            grown = dot3(split(fill), cut(qf_s, rows))
            later = grown if later is None else later + grown
        f_t = qf_t[here]
        back = f_t * (qfg - dot_right(pair_sum, split(f_t * qfg)))
        grad_q = grad_q + dot_left(split(back), queries[lo:hi])
        f = kf[rows]
        back = f * (kfg - dot_left(split(f * kfg), pair_sum))
        grad_k = grad_k + dot_right(ext_keys_t[:, lo:hi], split(back))
    half = grad_q.shape[0] // 2
    grad_k = grad_k.T
    return grad_q[:half] - grad_q[half:], grad_k[:half] - grad_k[half:]


def joined(pair):
    return pair[0].astype(f32) + pair[1].astype(f32)


def turned(x):
    eye = (iota((x.shape[1], x.shape[1]), 0) == iota((x.shape[1], x.shape[1]), 1)).astype(bf16)
    return dot_t(eye, x).astype(bf16)


def with_ones(x_t):
    return jnp.concatenate([x_t, (iota((PAD, x_t.shape[1]), 0) == 0).astype(bf16)], axis=0)


def pair_sums(features):
    half = features // 2
    return ((iota((features, features), 0) < half) == (iota((features, features), 1) < half)).astype(bf16)


def pack_kernel(queries_ref, keys_ref, values_ref, all_ref, keys_values_ref, queries_out_ref, queries_in, sems):
    rows = keys_ref.shape[0]
    first, second = pl.ds(0, rows), pl.ds(rows, rows)
    copies = [
        pltpu.make_async_copy(queries_ref, queries_in, sems.at[0]),
        pltpu.make_async_copy(keys_ref, all_ref.at[first], sems.at[1]),
        pltpu.make_async_copy(values_ref, all_ref.at[second], sems.at[2]),
        pltpu.make_async_copy(keys_ref, keys_values_ref.at[first], sems.at[3]),
        pltpu.make_async_copy(values_ref, keys_values_ref.at[second], sems.at[4]),
    ]
    for copy in copies:
        copy.start()
    copies[0].wait()
    for h in range(queries_ref.shape[1]):
        part = queries_in[:, h, :]
        all_ref[(2 + h) * rows : (3 + h) * rows] = part
        queries_out_ref[h * rows : (h + 1) * rows] = part
    for copy in copies[1:]:
        copy.wait()


def absorb_kernel(rows, parts, fresh, *refs):
    piece_refs, refs = refs[: len(parts)], refs[len(parts) :]
    query_weight_ref, key_weight_ref = refs[:2]
    buffers = refs[2:] if fresh else refs[8:]
    keys_ref, values_ref, _, kf_ref, _, _ = buffers
    if fresh:
        for ref in (keys_ref, values_ref):
            ref[:WINDOW] = jnp.zeros((WINDOW, ref.shape[1]), bf16)
        kf_ref[:, :WINDOW] = jnp.zeros((kf_ref.shape[0], WINDOW, kf_ref.shape[2]), bf16)
    take(rows, parts, piece_refs, query_weight_ref, key_weight_ref, buffers)


def take(rows, parts, piece_refs, query_weight_ref, key_weight_ref, buffers):
    place = lax.axis_index("seq")
    for (d, kind, _), ref in zip(parts, piece_refs):
        kv = (ref, 0) if kind in ("both", "kv") else None
        q = (ref, 2 if kind == "both" else 0) if kind in ("both", "q") else None
        absorb(rows, partner(place, d), kv, q, query_weight_ref, key_weight_ref, buffers)


def forward_kernel(rows, parts, *refs):
    piece_refs, refs = refs[: len(parts)], refs[len(parts) :]
    query_weight_ref, key_weight_ref = refs[:2]
    keys_ref, values_ref, queries_ref, kf_ref, qn_ref, qt_ref = buffers = refs[8:14]
    loss_ref, num_ref, den_ref = refs[14:]
    take(rows, parts, piece_refs, query_weight_ref, key_weight_ref, buffers)
    heads, tokens, width = queries_ref.shape
    block = block_of(tokens)
    values_t, aug_t = turned(values_ref[WINDOW:]), with_ones(turned(values_ref[:tokens]))
    total = jnp.zeros((1, 1), f32)
    for h in range(heads):
        kf_s = (kf_ref[h, :tokens, :width], kf_ref[h, :tokens, width:])
        loss, nums, dens = forward_pass(
            queries_ref[h], keys_ref[WINDOW:], kf_s, (qt_ref[h, :width], qt_ref[h, width:]), values_t, aug_t, block, tokens
        )
        total = total + loss
        for b in range(tokens // block):
            at = slice(b * block, (b + 1) * block)
            num_ref[h, :, at] = nums[b]
            den_ref[h, :, at] = jnp.broadcast_to(dens[b], (8, block))
    loss_ref[...] = jnp.broadcast_to(total / tokens, loss_ref.shape)


def partner(place, d):
    if d & 1:
        place = place + 1 - 2 * lax.rem(place, 2)
    if d & 2:
        place = lax.rem(place + 2, 4)
    return place


def block_of(tokens):
    return 256 if tokens % 256 == 0 else 128


def backward_kernel(keys_ref, values_ref, queries_ref, kf_ref, qn_ref, qt_ref, num_ref, den_ref, grad_q_ref, grad_k_ref):
    heads, tokens, width = queries_ref.shape
    block = block_of(tokens)
    cuts = [slice(b * block, (b + 1) * block) for b in range(tokens // block)]
    keys_t, sums = turned(keys_ref[:tokens]), pair_sums(width)
    for h in range(heads):
        grad_q_ref[h], grad_k_ref[h] = backward_pass(
            (kf_ref[h, :tokens, :width], kf_ref[h, :tokens, width:]), (qn_ref[h, :, :width], qn_ref[h, :, width:]),
            (qt_ref[h, :width], qt_ref[h, width:]), [num_ref[h, :, at] for at in cuts],
            [den_ref[h, :1, at] for at in cuts], queries_ref[h], values_ref[:tokens], keys_t, sums, block,
        )


def add_kernel(*refs):
    refs[-1][0] = sum(ref[0, 0] for ref in refs[:-1])


def local_gathered(queries, keys, values, query_weight, key_weight):
    rows, heads, width = queries.shape
    features = query_weight.shape[1]
    shards, columns = lax.axis_size("seq"), lax.axis_size("head")
    tokens = rows * shards
    vmem = pl.BlockSpec(memory_space=pltpu.VMEM)
    anywhere = pl.BlockSpec(memory_space=pl.ANY)
    shape = jax.ShapeDtypeStruct
    own, own_kv, own_q = pl.pallas_call(
        pack_kernel,
        out_shape=(
            shape(((2 + heads) * rows, width), bf16), shape((2 * rows, width), bf16), shape((heads * rows, width), bf16)
        ),
        in_specs=[pl.BlockSpec(memory_space=pltpu.HBM)] * 3,
        out_specs=(vmem,) * 3,
        scratch_shapes=[pltpu.VMEM(queries.shape, bf16), pltpu.SemaphoreType.DMA((5,))],
        compiler_params=pltpu.CompilerParams(vmem_limit_bytes=SMALL),
        name="pack",
    )(*(pltpu.with_memory_space_constraint(x, pltpu.HBM) for x in (queries, keys, values)))
    swap = lambda x, axis, size, d: lax.ppermute(x, axis, [(i, i ^ d) for i in range(size)])
    far_kv = swap(own_kv, "seq", shards, 2)
    far_q = swap(own_q, "seq", shards, 2)
    near = swap(own, "seq", shards, 1)
    last_kv = swap(far_kv, "seq", shards, 1)
    last_q = swap(far_q, "seq", shards, 1)
    buffers = (
        shape((tokens + WINDOW, width), bf16),
        shape((tokens + WINDOW, width), bf16),
        shape((heads, tokens, width), bf16),
        shape((heads, tokens + WINDOW, 4 * features), bf16),
        shape((heads, tokens, 4 * features), bf16),
        shape((heads, 4 * features, tokens), bf16),
    )

    def absorbed(parts, held):
        pieces = [piece for _, _, piece in parts]
        first = len(pieces) + 2
        return pl.pallas_call(
            functools.partial(absorb_kernel, rows, [(d, kind, None) for d, kind, _ in parts], not held),
            out_shape=buffers,
            in_specs=[vmem] * (first + len(held)),
            out_specs=(vmem,) * 6,
            input_output_aliases={first + i: i for i in range(len(held))},
            compiler_params=pltpu.CompilerParams(vmem_limit_bytes=SMALL),
            cost_estimate=pl.CostEstimate(flops=10**8, bytes_accessed=10**6, transcendentals=10**5),
        )(*pieces, query_weight, key_weight, *held)

    held = absorbed([(0, "both", own)], ())
    held = absorbed([(2, "kv", far_kv), (2, "q", far_q)], held)
    held = absorbed([(1, "both", near), (3, "kv", last_kv)], held)
    *held, loss, num, den = pl.pallas_call(
        functools.partial(forward_kernel, rows, [(3, "q", None)]),
        out_shape=buffers + (shape((8, 128), f32), shape((heads, width, tokens), f32), shape((heads, 8, tokens), f32)),
        in_specs=[vmem] * 9,
        out_specs=(vmem,) * 9,
        input_output_aliases={3 + i: i for i in range(6)},
        compiler_params=pltpu.CompilerParams(vmem_limit_bytes=LARGE),
        cost_estimate=pl.CostEstimate(flops=10**9, bytes_accessed=10**7, transcendentals=10**6),
        name="forward",
    )(last_q, query_weight, key_weight, *held)
    losses = [loss] + [swap(loss, "head", columns, d) for d in range(1, columns)]
    grad_query, grad_key = pl.pallas_call(
        backward_kernel,
        out_shape=(shape((heads, features, width), f32),) * 2,
        in_specs=[vmem] * 8,
        out_specs=(vmem,) * 2,
        compiler_params=pltpu.CompilerParams(vmem_limit_bytes=LARGE),
        cost_estimate=pl.CostEstimate(flops=10**9, bytes_accessed=10**7, transcendentals=10**6),
        name="backward",
    )(*held, num, den)
    loss = pl.pallas_call(
        add_kernel,
        out_shape=shape((1,), f32),
        in_specs=[vmem] * columns,
        out_specs=pl.BlockSpec(memory_space=pltpu.SMEM),
        compiler_params=pltpu.CompilerParams(vmem_limit_bytes=SMALL),
        name="join",
    )(*losses)
    return loss, grad_query, grad_key


def local(queries, keys, values, query_weight, key_weight):
    rows, _, width = queries.shape
    shards = lax.axis_size("seq")
    columns = lax.axis_size("head")
    fits = shards == 4 and columns & (columns - 1) == 0 and rows == width == 128 and 2 * query_weight.shape[1] == width
    if fits:
        return local_gathered(queries, keys, values, query_weight, key_weight)
    return local_general(queries, keys, values, query_weight, key_weight)


def solution(mesh):
    in_specs = (
        P(("rep", "seq"), "head", None),
        P(("rep", "seq"), None),
        P(("rep", "seq"), None),
        P(("rep", "head"), None, None),
        P(("rep", "head"), None, None),
    )
    out_specs = (P("rep"), P(("rep", "head"), None, None), P(("rep", "head"), None, None))
    return jax.shard_map(local, mesh=mesh, in_specs=in_specs, out_specs=out_specs, check_vma=False)
```
